32 devices in a mesh: dp: 8 (over z, x), seq: 4 (over y, core).
Axes of the slice: x: 2, y: 2, z: 4, core: 2. Of those that a mesh axis runs over, the one named last changes fastest.
Arguments:
- tiles: bfloat16 [8, 1536, 1536], P('dp', 'seq'), may hold values from -24 to 24
- tile_counts: int32 [8, 4], P('dp'), may hold values from 96 to 384, as said below
- norm_gain: float32 [1536], replicated, may hold values from 0.5 to 8
- qkv_weight: bfloat16 [1536, 2304], P('dp'), may hold values from -1 to 1
Outputs:
- context: bfloat16 [8, 1536, 768], P('dp', 'seq')
The draws below stay inside these ranges and needn't reach their ends.
Inputs may be any that keep to these rules, and one draw needn't show every extreme that they name: `tile_counts`: every slide has one block with exactly 384 tissue tiles.
All inputs are finite; a program needn't handle non-finite values.
Results may differ from the reference program's by a relative error of at most 0.017.
The reference program's roundings to bfloat16 on the way (of `normed` and `qkv`) count: a program that leaves them out, or rounds other values in their place, can miss the bound.
Values may be sent and summed in bfloat16 or wider, within the bound.
No kernel may reach another device: no remote copies, remote signals or barrier semaphores. Data moves between devices by JAX's collectives and lax.ppermute only.
A program may use at most 64 MiB of HBM per device.

```python
import jax
import jax.numpy as jnp
from jax import lax

D = 1536
HEADS = 6
HD = 128
TOK_DEV = 384
MID_RATE = 4
SEQ_LEN = 1536
SLIDES = 8
N_SEQ = 4


def draw_tile_counts(key, part):
    first_key, second_key, third_key = jax.random.split(key, 3)
    first_draw = jax.random.randint(first_key, (SLIDES, N_SEQ), TOK_DEV // 4, TOK_DEV + 1)
    second_draw = jax.random.randint(second_key, (SLIDES, N_SEQ), TOK_DEV // 4, TOK_DEV + 1)
    base_counts = jnp.minimum(first_draw, second_draw)
    full_block = jax.random.randint(third_key, (SLIDES, 1), 0, N_SEQ)
    blocks = jnp.arange(N_SEQ, dtype=jnp.int32)[None, :]
    return jnp.where(blocks == full_block, TOK_DEV, base_counts).astype(jnp.int32)


def draw_norm_gain(key, part):
    return jax.random.uniform(key, (D,), jnp.float32, 0.5, 2.0)


def draw_tiles(key, part):

    def one_slide(slide_idx):
        slide_key = jax.random.fold_in(key, slide_idx + 100)
        rough_part = jax.random.truncated_normal(jax.random.fold_in(slide_key, 1), -6.0, 6.0, (SEQ_LEN, D), jnp.float32)
        return rough_part.astype(jnp.bfloat16)
    return lax.map(one_slide, jnp.arange(SLIDES, dtype=jnp.int32))


def draw_qkv_weight(key, part):
    width = HEADS * HD
    matrix = jax.random.truncated_normal(jax.random.fold_in(key, 1), -6.0, 6.0, (D, 3 * width), jnp.float32) * D ** (-0.5)
    return jnp.clip(matrix, -1.0, 1.0).astype(jnp.bfloat16)


def setup_inputs(seed: int = 0) -> dict:
    streams_of = jax.random.split(jax.random.key(seed), 5)
    return {
        "tiles": draw_tiles(jax.random.fold_in(streams_of[4], 71), 0),
        "tile_counts": draw_tile_counts(jax.random.fold_in(streams_of[4], 71), 0),
        "norm_gain": draw_norm_gain(jax.random.fold_in(streams_of[4], 71), 0),
        "qkv_weight": draw_qkv_weight(jax.random.fold_in(streams_of[4], 71), 0),
    }


NEG = -1e+30
EPS = 1e-05

def layer_norm(rows_in, gain):
    floats = rows_in.astype(jnp.float32)
    center = floats - lax.optimization_barrier(jnp.mean(floats, axis=-1, keepdims=True))
    spread_sq = lax.optimization_barrier(jnp.mean(center * center, axis=-1, keepdims=True))
    return (center * lax.rsqrt(spread_sq + EPS) * gain).astype(jnp.bfloat16)

def sample_rows(array, stride):
    shaped = array.reshape((array.shape[0] // stride, stride) + array.shape[1:])
    return jnp.stack([shaped[:, head_idx % stride, head_idx] for head_idx in range(array.shape[1])])

def attend(queries, keys, values_in, key_live, scale):
    scores = jnp.einsum('hsqd,hskd->hsqk', queries.astype(jnp.float32), keys.astype(jnp.float32)) * scale
    scores = jnp.where(key_live[:, :, None, :], scores, NEG)
    top = lax.optimization_barrier(jnp.max(scores, axis=-1))
    expo = jnp.exp(scores - top[..., None])
    denom = lax.optimization_barrier(jnp.sum(expo, axis=-1))
    weights = (expo / denom[..., None]).astype(jnp.bfloat16)
    result = jnp.einsum('hsqk,hskd->hsqd', weights.astype(jnp.float32), values_in.astype(jnp.float32))
    return (result, top + jnp.log(denom))

def spread(result, log_total, stride):
    heads_n = result.shape[0]
    count_n = result.shape[1]
    onehot = jnp.arange(stride, dtype=jnp.int32)[None, :] == (jnp.arange(heads_n, dtype=jnp.int32) % stride)[:, None]
    full_ctx = (result[:, :, None, :] * onehot[:, None, :, None].astype(result.dtype)).reshape(heads_n, count_n * stride, result.shape[2])
    chosen = jnp.broadcast_to(onehot[:, None, :], (heads_n, count_n, stride)).reshape(heads_n, count_n * stride)
    full_lt = jnp.where(chosen, jnp.repeat(log_total, stride, axis=1), NEG)
    return (full_ctx, full_lt)

def combine(contexts, totals):
    stacked_lt = jnp.stack(totals)
    top = lax.optimization_barrier(jnp.max(stacked_lt, axis=0))
    wts = jnp.exp(stacked_lt - top)
    stacked_ctx = jnp.stack(contexts)
    return lax.optimization_barrier(jnp.sum(wts[..., None] * stacked_ctx, axis=0)) / lax.optimization_barrier(jnp.sum(wts, axis=0))[..., None]

def reference(tiles, tile_counts, norm_gain, qkv_weight):
    width = HEADS * HD
    scale = HD ** (-0.5)

    def one_slide(inputs):
        slide_tiles, slide_counts = inputs
        length = slide_tiles.shape[0]
        is_live = jnp.arange(length, dtype=jnp.int32) % TOK_DEV < jnp.repeat(slide_counts, TOK_DEV, total_repeat_length=length)
        normed = layer_norm(slide_tiles, norm_gain)
        qkv = jnp.dot(normed, qkv_weight, preferred_element_type=jnp.float32).astype(jnp.bfloat16)
        queries = qkv[:, :width].reshape(length, HEADS, HD)
        keys = qkv[:, width:2 * width].reshape(length, HEADS, HD)
        values_in = qkv[:, 2 * width:].reshape(length, HEADS, HD)
        contexts = []
        totals = []
        for span, stride in ((TOK_DEV, 1), (MID_RATE * TOK_DEV, MID_RATE), (SEQ_LEN, N_SEQ)):
            segs = length // span
            per_seg = span // stride
            q_samp = sample_rows(queries, stride).reshape(HEADS, segs, per_seg, HD)
            k_samp = sample_rows(keys, stride).reshape(HEADS, segs, per_seg, HD)
            v_samp = sample_rows(values_in, stride).reshape(HEADS, segs, per_seg, HD)
            live_rows = is_live.reshape(length // stride, stride)
            live_samp = jnp.stack([live_rows[:, head_idx % stride] for head_idx in range(HEADS)]).reshape(HEADS, segs, per_seg)
            result, log_total = attend(q_samp, k_samp, v_samp, live_samp, scale)
            full_ctx, full_lt = spread(result.reshape(HEADS, length // stride, HD), log_total.reshape(HEADS, length // stride), stride)
            contexts.append(full_ctx)
            totals.append(full_lt)
        mixed = combine(contexts, totals)
        mixed = jnp.where(is_live[None, :, None], mixed, 0.0)
        return mixed.transpose(1, 0, 2).reshape(length, width).astype(jnp.bfloat16)
    return lax.map(one_slide, (tiles, tile_counts))
```

```python
import functools
import math

import jax
import jax.numpy as jnp
from jax import lax
from jax.experimental import pallas as pl
from jax.experimental.pallas import tpu as pltpu
from jax.sharding import PartitionSpec as P

HEADS = 6
MID_RATE = 4


NEG = -1e30
EPS = 1e-05


def from_partner(value, axis, bit):
    mask = 2**bit
    pairs = [(source, source ^ mask) for source in range(lax.axis_size(axis))]
    return lax.ppermute(value, axis, pairs)


def layer_norm(rows_in, gain):
    floats = rows_in.astype(jnp.float32)
    center = floats - jnp.mean(floats, axis=-1, keepdims=True)
    spread_sq = jnp.mean(center * center, axis=-1, keepdims=True)
    return (center * lax.rsqrt(spread_sq + EPS) * gain).astype(jnp.bfloat16)


def sample_rows(array, stride):
    shaped = array.reshape((array.shape[0] // stride, stride) + array.shape[1:])
    return jnp.stack([shaped[:, head_idx % stride, head_idx] for head_idx in range(array.shape[1])])


def attend(queries, keys, values_in, key_live, scale):
    scores = (
        jnp.einsum("hsqd,hskd->hsqk", queries, keys, preferred_element_type=jnp.float32) * scale
    )
    scores = jnp.where(key_live[:, :, None, :], scores, NEG)
    top = jnp.max(scores, axis=-1)
    expo = jnp.exp(scores - top[..., None])
    denom = jnp.sum(expo, axis=-1)
    weights = (expo / denom[..., None]).astype(jnp.bfloat16)
    result = jnp.einsum("hsqk,hskd->hsqd", weights, values_in, preferred_element_type=jnp.float32)
    return (result, top + jnp.log(denom))


def spread(result, log_total, stride):
    heads_n = result.shape[0]
    count_n = result.shape[1]
    onehot = (
        jnp.arange(stride, dtype=jnp.int32)[None, :]
        == (jnp.arange(heads_n, dtype=jnp.int32) % stride)[:, None]
    )
    full_ctx = (result[:, :, None, :] * onehot[:, None, :, None].astype(result.dtype)).reshape(
        heads_n, count_n * stride, result.shape[2]
    )
    chosen = jnp.broadcast_to(onehot[:, None, :], (heads_n, count_n, stride)).reshape(
        heads_n, count_n * stride
    )
    full_lt = jnp.where(chosen, jnp.repeat(log_total, stride, axis=1), NEG)
    return (full_ctx, full_lt)


def combine(contexts, totals):
    stacked_lt = jnp.stack(totals)
    top = jnp.max(stacked_lt, axis=0)
    wts = jnp.exp(stacked_lt - top)
    stacked_ctx = jnp.stack(contexts)
    return jnp.sum(wts[..., None] * stacked_ctx, axis=0) / jnp.sum(wts, axis=0)[..., None]


def key_alive(owners, within, counts, stride, heads_n):
    seq_n = counts.shape[0]
    owner_count = jnp.sum(
        jnp.where(
            owners[:, None] == jnp.arange(seq_n, dtype=jnp.int32)[None, :], counts[None, :], 0
        ),
        axis=1,
    )
    offsets = jnp.arange(heads_n, dtype=jnp.int32) % stride
    slots = offsets[:, None] + stride * within[None, :]
    return slots < owner_count[None, :]


def sampled_attention(queries, gathered, alive, stride, scale):
    heads_n = queries.shape[0]
    per_dev = queries.shape[1]
    result, log_total = attend(
        queries[:, None], gathered[0][:, None], gathered[1][:, None], alive[:, None], scale
    )
    return spread(
        result.reshape(heads_n, per_dev, result.shape[3]),
        log_total.reshape(heads_n, per_dev),
        stride,
    )


def local(tiles, tile_counts, norm_gain, qkv_weight):
    rows_in = tiles[0]
    counts = tile_counts[0]
    tok_dev = rows_in.shape[0]
    seq_n = lax.axis_size("seq")
    my_index = lax.axis_index("seq")
    dev_ids = jnp.arange(seq_n, dtype=jnp.int32)
    my_count = jnp.sum(jnp.where(dev_ids == my_index, counts, 0))
    is_live = jnp.arange(tok_dev, dtype=jnp.int32) < my_count
    normed = layer_norm(rows_in, norm_gain)
    width3 = qkv_weight.shape[1]
    width = width3 // 3
    heads_n = HEADS
    head_dim = width // heads_n
    scale = head_dim ** (-0.5)
    qkv = jnp.dot(
        normed,
        lax.all_gather(qkv_weight, "dp", axis=0, tiled=True),
        preferred_element_type=jnp.float32,
    ).astype(jnp.bfloat16)
    queries = qkv[:, :width].reshape(tok_dev, heads_n, head_dim)
    keys = qkv[:, width : 2 * width].reshape(tok_dev, heads_n, head_dim)
    values_in = qkv[:, 2 * width :].reshape(tok_dev, heads_n, head_dim)
    local_live = jnp.broadcast_to(is_live[None, None, :], (heads_n, 1, tok_dev))
    local_ctx, local_lt = attend(
        queries.transpose(1, 0, 2)[:, None],
        keys.transpose(1, 0, 2)[:, None],
        values_in.transpose(1, 0, 2)[:, None],
        local_live,
        scale,
    )
    local_ctx = local_ctx.reshape(heads_n, tok_dev, head_dim)
    local_lt = local_lt.reshape(heads_n, tok_dev)
    mid_stride = MID_RATE
    mid_rows = tok_dev // mid_stride
    q_mid = sample_rows(queries, mid_stride)
    kv_mid = jnp.stack([sample_rows(keys, mid_stride), sample_rows(values_in, mid_stride)])
    bit_count = MID_RATE.bit_length() - 1
    bit_order = list(range(bit_count))
    mid_keys = kv_mid
    source_ids = jnp.reshape(my_index, (1,))
    for bit_pos in bit_order:
        partner_keys = from_partner(mid_keys, "seq", bit_pos)
        mid_keys = jnp.concatenate([mid_keys, partner_keys], axis=2)
        source_ids = jnp.concatenate([source_ids, source_ids ^ 1 << bit_pos])
    mid_owners = jnp.repeat(source_ids, mid_rows, total_repeat_length=mid_stride * mid_rows)
    mid_within = jnp.tile(jnp.arange(mid_rows, dtype=jnp.int32), mid_stride)
    mid_alive = key_alive(mid_owners, mid_within, counts, mid_stride, heads_n)
    mid_ctx, mid_lt = sampled_attention(q_mid, mid_keys, mid_alive, mid_stride, scale)
    wide_rows = tok_dev // seq_n
    q_wide = sample_rows(queries, seq_n)
    kv_wide = jnp.stack([sample_rows(keys, seq_n), sample_rows(values_in, seq_n)])
    wide_keys = lax.all_gather(kv_wide, "seq", axis=2, tiled=True)
    wide_owners = jnp.arange(seq_n * wide_rows, dtype=jnp.int32) // wide_rows
    wide_within = jnp.arange(seq_n * wide_rows, dtype=jnp.int32) % wide_rows
    wide_alive = key_alive(wide_owners, wide_within, counts, seq_n, heads_n)
    wide_ctx, wide_lt = sampled_attention(q_wide, wide_keys, wide_alive, seq_n, scale)
    mixed = combine([local_ctx, mid_ctx, wide_ctx], [local_lt, mid_lt, wide_lt])
    mixed = jnp.where(is_live[None, :, None], mixed, 0.0)
    return mixed.transpose(1, 0, 2).reshape(tok_dev, width).astype(jnp.bfloat16)[None]


def pair_order(move):
    dp_n = lax.axis_size("dp")
    seq_n = lax.axis_size("seq")
    pairs = []
    for row in range(dp_n):
        for col in range(seq_n):
            to_row, to_col = move(row, col)
            pairs.append((row * seq_n + col, to_row * seq_n + to_col))
    return pairs


def route(value, move):
    return lax.ppermute(value, ("dp", "seq"), pair_order(move))


def core_swap(value):
    return route(value, lambda row, col: (row, col ^ 1))


def chip_swap(value):
    return route(value, lambda row, col: (row, col ^ 2))


def my_half():
    return lax.axis_index("seq") // 2


def my_core():
    return lax.axis_index("seq") % 2


def norm_kernel(rows_ref, gain_ref, out_ref):
    out_ref[...] = layer_norm(rows_ref[...], gain_ref[...])


def norm_rows(rows_in, gain, start, count):
    width = rows_in.shape[1]
    block = start // count
    return pl.pallas_call(
        norm_kernel,
        grid=(1,),
        in_specs=[
            pl.BlockSpec((count, width), lambda step: (block, 0)),
            pl.BlockSpec((1, width), lambda step: (0, 0)),
        ],
        out_specs=pl.BlockSpec((count, width), lambda step: (0, 0)),
        out_shape=jax.ShapeDtypeStruct((count, width), jnp.bfloat16),
        cost_estimate=pl.CostEstimate(
            flops=8 * count * width, transcendentals=count, bytes_accessed=4 * count * width
        ),
        name="norm_rows",
    )(rows_in, gain)


def columns_kernel(weight_ref, mine_ref, part_ref, sems):
    rows_n, cols_n = mine_ref.shape
    part_n = part_ref.shape[0]
    third = cols_n // 3
    half = my_half()
    copies = []
    for kind in range(3):
        start = pl.multiple_of((2 * kind + half) * third, third)
        copies.append(
            pltpu.make_async_copy(
                weight_ref.at[:, pl.ds(start, third)],
                mine_ref.at[:, pl.ds(kind * third, third)],
                sems.at[kind],
            )
        )
    for copy in copies:
        copy.start()
    for copy in copies:
        copy.wait()
    first = pl.multiple_of(my_core() * part_n, part_n)
    part_ref[...] = mine_ref[pl.ds(first, part_n), :]


def my_columns(weight):
    rows_n, width3 = weight.shape
    cols_n = width3 // 2
    return pl.pallas_call(
        columns_kernel,
        in_specs=[pl.BlockSpec(memory_space=pl.ANY)],
        out_specs=[pl.BlockSpec(memory_space=pltpu.VMEM)] * 2,
        out_shape=[
            jax.ShapeDtypeStruct((rows_n, cols_n), weight.dtype),
            jax.ShapeDtypeStruct((rows_n // 2, cols_n), weight.dtype),
        ],
        scratch_shapes=[pltpu.SemaphoreType.DMA((3,))],
        cost_estimate=pl.CostEstimate(
            flops=0, transcendentals=0, bytes_accessed=5 * rows_n * cols_n
        ),
        name="my_columns",
    )(weight)


def gather_columns(weight):
    own, part = my_columns(weight)
    near = route(own, lambda row, col: (row ^ (4 if col & 1 else 2), col))
    side = route(part, lambda row, col: (row ^ 1, col))
    cross = route(near, lambda row, col: (row ^ 1, col))
    far = route(near, lambda row, col: (row ^ (2 if col & 1 else 0), col))
    corner = route(side, lambda row, col: (row ^ 6, col))
    return (
        own,
        near,
        core_swap(near),
        cross,
        core_swap(cross),
        far,
        core_swap(far),
        side,
        core_swap(side),
        corner,
        core_swap(corner),
    )


def project_kernel(chunks_n, *refs):
    chunks = refs[:chunks_n]
    own, near, near2, cross, cross2, far, far2, side, side2, corner, corner2 = refs[
        chunks_n : chunks_n + 11
    ]
    out_ref, samp_ref, rows_scr, weight_scr, total_scr, sems = refs[chunks_n + 11 :]
    shard = own.shape[0]
    part = side.shape[0]
    mine = lax.axis_index("dp")
    core = my_core()
    half = my_half()

    def shard_at(mask):
        return pl.multiple_of(jnp.bitwise_xor(mine, mask) * shard, shard)

    copies = []
    start = 0
    for chunk in chunks:
        rows_n = chunk.shape[0]
        copies.append((chunk, rows_scr.at[pl.ds(start, rows_n), :]))
        start += rows_n

    def put(source, first):
        copies.append((source, weight_scr.at[pl.ds(first, source.shape[0]), :]))

    put(own, shard_at(0))
    put(near, shard_at(2 + 2 * core))
    put(near2, shard_at(4 - 2 * core))
    put(cross, shard_at(3 + 2 * core))
    put(cross2, shard_at(5 - 2 * core))
    low = core * part
    high = part - core * part
    put(side, pl.multiple_of(shard_at(1) + low, part))
    put(side2, pl.multiple_of(shard_at(1) + high, part))
    put(corner, pl.multiple_of(shard_at(7) + low, part))
    put(corner2, pl.multiple_of(shard_at(7) + high, part))
    handles = []
    for pos, (source, target) in enumerate(copies):
        handles.append(pltpu.make_async_copy(source, target, sems.at[pos]))
        handles[-1].start()
    far_at = weight_scr.at[pl.ds(shard_at(6), shard), :]

    @pl.when(core == 1)
    def _():
        pltpu.make_async_copy(far, far_at, sems.at[len(copies)]).start()

    @pl.when(core == 0)
    def _():
        pltpu.make_async_copy(far2, far_at, sems.at[len(copies)]).start()

    handles.append(pltpu.make_async_copy(far, far_at, sems.at[len(copies)]))
    for handle in handles:
        handle.wait()
    total = jnp.dot(rows_scr[...], weight_scr[...], preferred_element_type=jnp.float32)
    out_ref[...] = total.astype(jnp.bfloat16)
    _, heads_n, samp_n, head_dim = samp_ref.shape
    stride = total.shape[0] // samp_n
    for kind in range(3):
        for head in range(heads_n):
            slot = kind * heads_n + head
            total_scr[slot] = total[:, slot * head_dim : (slot + 1) * head_dim]
            offset = lax.rem(half * heads_n + head, stride)
            samp_ref[kind, head] = total_scr.at[slot][
                pl.ds(offset, samp_n, stride=stride), :
            ].astype(jnp.bfloat16)


def project(chunks, pieces, heads_n, stride):
    rows_n = sum(chunk.shape[0] for chunk in chunks)
    depth = chunks[0].shape[1]
    cols_n = pieces[0].shape[1]
    head_dim = cols_n // (3 * heads_n)
    return pl.pallas_call(
        functools.partial(project_kernel, len(chunks)),
        in_specs=[pl.BlockSpec(memory_space=pl.ANY)] * (len(chunks) + len(pieces)),
        out_specs=[pl.BlockSpec(memory_space=pltpu.VMEM)] * 2,
        out_shape=[
            jax.ShapeDtypeStruct((rows_n, cols_n), jnp.bfloat16),
            jax.ShapeDtypeStruct((3, heads_n, rows_n // stride, head_dim), jnp.bfloat16),
        ],
        scratch_shapes=[
            pltpu.VMEM((rows_n, depth), jnp.bfloat16),
            pltpu.VMEM((depth, cols_n), jnp.bfloat16),
            pltpu.VMEM((3 * heads_n, rows_n, head_dim), jnp.float32),
            pltpu.SemaphoreType.DMA((len(chunks) + 10,)),
        ],
        cost_estimate=pl.CostEstimate(
            flops=2 * rows_n * depth * cols_n,
            transcendentals=0,
            bytes_accessed=2 * (rows_n * depth + depth * cols_n + rows_n * cols_n),
        ),
        name="project",
    )(*chunks, *pieces)


def row_times(left, right):
    return lax.dot_general(
        left, right, (((1,), (1,)), ((), ())), preferred_element_type=jnp.float32
    )


def attend_kernel(
    stride, mine_first, counts_ref, qkv_ref, samp_ref, other_ref, remote_ref, out_ref, full_scr
):
    tok_dev, cols_n = qkv_ref.shape
    _, heads_n, samp_n, head_dim = samp_ref.shape
    width = cols_n // 3
    half = my_half()
    seq_index = lax.axis_index("seq")
    block = seq_index if mine_first else jnp.bitwise_xor(seq_index, 2)
    factor = head_dim ** (-0.5) * math.log2(math.e)
    live_n = counts_ref[0, block]
    key_slot = lax.broadcasted_iota(jnp.int32, (1, tok_dev), 1)
    local_bias = jnp.where(key_slot < live_n, 0.0, NEG)
    row_live = lax.broadcasted_iota(jnp.int32, (tok_dev, head_dim), 0) < live_n
    samp_slot = lax.broadcasted_iota(jnp.int32, (1, samp_n), 1)
    owners = [
        block,
        jnp.bitwise_xor(block, 2),
        jnp.bitwise_xor(seq_index, 1),
        jnp.bitwise_xor(seq_index, 3),
    ]
    for head in range(heads_n):
        cols = slice(head * head_dim, (head + 1) * head_dim)
        query = qkv_ref[:, cols]
        key = qkv_ref[:, width + head * head_dim : width + (head + 1) * head_dim]
        value = qkv_ref[:, 2 * width + head * head_dim : 2 * width + (head + 1) * head_dim]
        scores = row_times(query, key) + local_bias
        top = jnp.max(scores, axis=-1, keepdims=True)
        expo = jnp.exp2((scores - top) * factor)
        denom = jnp.sum(expo, axis=-1, keepdims=True)
        result = jnp.dot(expo.astype(jnp.bfloat16), value, preferred_element_type=jnp.float32)
        full_scr[...] = result / denom
        offset = lax.rem(half * heads_n + head, stride)
        live_parts = []
        for owner in owners:
            slots = offset + stride * samp_slot
            live_parts.append(jnp.where(slots < counts_ref[0, owner], 0.0, NEG))
        samp_bias = jnp.concatenate(live_parts, axis=1)
        samp_query = samp_ref[0, head]
        samp_keys = jnp.concatenate(
            [samp_ref[1, head], other_ref[1, head], remote_ref[0, 0, head], remote_ref[1, 0, head]]
        )
        samp_values = jnp.concatenate(
            [samp_ref[2, head], other_ref[2, head], remote_ref[0, 1, head], remote_ref[1, 1, head]]
        )
        near_scores = row_times(samp_query, key) + local_bias
        wide_scores = row_times(samp_query, samp_keys) + samp_bias
        top = jnp.maximum(
            jnp.max(near_scores, axis=-1, keepdims=True),
            jnp.max(wide_scores, axis=-1, keepdims=True),
        )
        near = jnp.exp2((near_scores - top) * factor)
        wide = jnp.exp2((wide_scores - top) * factor)
        denom = jnp.sum(near, axis=-1, keepdims=True) + 2.0 * jnp.sum(
            wide, axis=-1, keepdims=True
        )
        result = jnp.dot(
            near.astype(jnp.bfloat16), value, preferred_element_type=jnp.float32
        ) + 2.0 * jnp.dot(
            wide.astype(jnp.bfloat16), samp_values, preferred_element_type=jnp.float32
        )
        full_scr[pl.ds(offset, samp_n, stride=stride), :] = result / denom
        out_ref[:, cols] = jnp.where(row_live, full_scr[...], 0.0).astype(jnp.bfloat16)


def attend_block(counts, qkv, samp, other, remote, stride, mine_first):
    tok_dev, cols_n = qkv.shape
    _, heads_n, samp_n, head_dim = samp.shape
    return pl.pallas_call(
        functools.partial(attend_kernel, stride, mine_first),
        in_specs=[pl.BlockSpec(memory_space=pltpu.SMEM)]
        + [pl.BlockSpec(memory_space=pltpu.VMEM)] * 4,
        out_specs=pl.BlockSpec(memory_space=pltpu.VMEM),
        out_shape=jax.ShapeDtypeStruct((tok_dev, cols_n // 3), jnp.bfloat16),
        scratch_shapes=[pltpu.VMEM((tok_dev, head_dim), jnp.float32)],
        cost_estimate=pl.CostEstimate(
            flops=5 * heads_n * tok_dev * tok_dev * head_dim,
            transcendentals=2 * heads_n * tok_dev * tok_dev,
            bytes_accessed=2 * tok_dev * cols_n,
        ),
        name="attend_mine" if mine_first else "attend_other",
    )(counts, qkv, samp, other, remote)


def join_kernel(mine_ref, other_ref, out_ref):
    width = mine_ref.shape[1]
    half = my_half()
    mine_at = pl.multiple_of(half * width, width)
    other_at = pl.multiple_of((1 - half) * width, width)
    out_ref[:, pl.ds(mine_at, width)] = mine_ref[...]
    out_ref[:, pl.ds(other_at, width)] = other_ref[...]


def join_halves(mine, other):
    rows_n, width = mine.shape
    return pl.pallas_call(
        join_kernel,
        in_specs=[pl.BlockSpec(memory_space=pltpu.VMEM)] * 2,
        out_specs=pl.BlockSpec(memory_space=pltpu.VMEM),
        out_shape=jax.ShapeDtypeStruct((rows_n, 2 * width), mine.dtype),
        cost_estimate=pl.CostEstimate(
            flops=0, transcendentals=0, bytes_accessed=8 * rows_n * width
        ),
        name="join_halves",
    )(mine, other)


CHUNKS = 3


def local_paired(tiles, tile_counts, norm_gain, qkv_weight):
    rows_in = tiles[0]
    tok_dev = rows_in.shape[0]
    stride = MID_RATE
    heads_n = HEADS // 2
    gain = norm_gain[None]
    count = tok_dev // CHUNKS
    mine = [norm_rows(rows_in, gain, start, count) for start in range(0, tok_dev, count)]
    other = [chip_swap(chunk) for chunk in mine]
    pieces = gather_columns(qkv_weight)
    qkv, samp = project(mine, pieces, heads_n, stride)
    qkv2, samp2 = project(other, pieces, heads_n, stride)
    remote = core_swap(jnp.stack([samp[1:], samp2[1:]]))
    back = chip_swap(attend_block(tile_counts, qkv2, samp2, samp, remote, stride, False))
    kept = attend_block(tile_counts, qkv, samp, samp2, remote, stride, True)
    return join_halves(kept, back)[None]


def solution(mesh):
    paired = (
        mesh.shape["seq"] == MID_RATE == 4 and mesh.shape["dp"] == 8 and HEADS % 2 == 0
    )
    return jax.shard_map(
        local_paired if paired else local,
        mesh=mesh,
        in_specs=(P("dp", "seq", None), P("dp", None), P(), P("dp", None)),
        out_specs=P("dp", "seq", None),
        check_vma=False,
    )
```

```python
import functools
import math

import jax
import jax.numpy as jnp
from jax import lax
from jax.experimental import pallas as pl
from jax.experimental.pallas import tpu as pltpu
from jax.sharding import PartitionSpec as P

HEADS = 6
MID_RATE = 4


NEG = -1e30
EPS = 1e-05


def from_partner(value, axis, bit):
    mask = 2**bit
    pairs = [(source, source ^ mask) for source in range(lax.axis_size(axis))]
    return lax.ppermute(value, axis, pairs)


def layer_norm(rows_in, gain):
    floats = rows_in.astype(jnp.float32)
    center = floats - jnp.mean(floats, axis=-1, keepdims=True)
    spread_sq = jnp.mean(center * center, axis=-1, keepdims=True)
    return (center * lax.rsqrt(spread_sq + EPS) * gain).astype(jnp.bfloat16)


def sample_rows(array, stride):
    shaped = array.reshape((array.shape[0] // stride, stride) + array.shape[1:])
    return jnp.stack([shaped[:, head_idx % stride, head_idx] for head_idx in range(array.shape[1])])


def attend(queries, keys, values_in, key_live, scale):
    scores = (
        jnp.einsum("hsqd,hskd->hsqk", queries, keys, preferred_element_type=jnp.float32) * scale
    )
    scores = jnp.where(key_live[:, :, None, :], scores, NEG)
    top = jnp.max(scores, axis=-1)
    expo = jnp.exp(scores - top[..., None])
    denom = jnp.sum(expo, axis=-1)
    weights = (expo / denom[..., None]).astype(jnp.bfloat16)
    result = jnp.einsum("hsqk,hskd->hsqd", weights, values_in, preferred_element_type=jnp.float32)
    return (result, top + jnp.log(denom))


def spread(result, log_total, stride):
    heads_n = result.shape[0]
    count_n = result.shape[1]
    onehot = (
        jnp.arange(stride, dtype=jnp.int32)[None, :]
        == (jnp.arange(heads_n, dtype=jnp.int32) % stride)[:, None]
    )
    full_ctx = (result[:, :, None, :] * onehot[:, None, :, None].astype(result.dtype)).reshape(
        heads_n, count_n * stride, result.shape[2]
    )
    chosen = jnp.broadcast_to(onehot[:, None, :], (heads_n, count_n, stride)).reshape(
        heads_n, count_n * stride
    )
    full_lt = jnp.where(chosen, jnp.repeat(log_total, stride, axis=1), NEG)
    return (full_ctx, full_lt)


def combine(contexts, totals):
    stacked_lt = jnp.stack(totals)
    top = jnp.max(stacked_lt, axis=0)
    wts = jnp.exp(stacked_lt - top)
    stacked_ctx = jnp.stack(contexts)
    return jnp.sum(wts[..., None] * stacked_ctx, axis=0) / jnp.sum(wts, axis=0)[..., None]


def key_alive(owners, within, counts, stride, heads_n):
    seq_n = counts.shape[0]
    owner_count = jnp.sum(
        jnp.where(
            owners[:, None] == jnp.arange(seq_n, dtype=jnp.int32)[None, :], counts[None, :], 0
        ),
        axis=1,
    )
    offsets = jnp.arange(heads_n, dtype=jnp.int32) % stride
    slots = offsets[:, None] + stride * within[None, :]
    return slots < owner_count[None, :]


def sampled_attention(queries, gathered, alive, stride, scale):
    heads_n = queries.shape[0]
    per_dev = queries.shape[1]
    result, log_total = attend(
        queries[:, None], gathered[0][:, None], gathered[1][:, None], alive[:, None], scale
    )
    return spread(
        result.reshape(heads_n, per_dev, result.shape[3]),
        log_total.reshape(heads_n, per_dev),
        stride,
    )


def local(tiles, tile_counts, norm_gain, qkv_weight):
    rows_in = tiles[0]
    counts = tile_counts[0]
    tok_dev = rows_in.shape[0]
    seq_n = lax.axis_size("seq")
    my_index = lax.axis_index("seq")
    dev_ids = jnp.arange(seq_n, dtype=jnp.int32)
    my_count = jnp.sum(jnp.where(dev_ids == my_index, counts, 0))
    is_live = jnp.arange(tok_dev, dtype=jnp.int32) < my_count
    normed = layer_norm(rows_in, norm_gain)
    width3 = qkv_weight.shape[1]
    width = width3 // 3
    heads_n = HEADS
    head_dim = width // heads_n
    scale = head_dim ** (-0.5)
    qkv = jnp.dot(
        normed,
        lax.all_gather(qkv_weight, "dp", axis=0, tiled=True),
        preferred_element_type=jnp.float32,
    ).astype(jnp.bfloat16)
    queries = qkv[:, :width].reshape(tok_dev, heads_n, head_dim)
    keys = qkv[:, width : 2 * width].reshape(tok_dev, heads_n, head_dim)
    values_in = qkv[:, 2 * width :].reshape(tok_dev, heads_n, head_dim)
    local_live = jnp.broadcast_to(is_live[None, None, :], (heads_n, 1, tok_dev))
    local_ctx, local_lt = attend(
        queries.transpose(1, 0, 2)[:, None],
        keys.transpose(1, 0, 2)[:, None],
        values_in.transpose(1, 0, 2)[:, None],
        local_live,
        scale,
    )
    local_ctx = local_ctx.reshape(heads_n, tok_dev, head_dim)
    local_lt = local_lt.reshape(heads_n, tok_dev)
    mid_stride = MID_RATE
    mid_rows = tok_dev // mid_stride
    q_mid = sample_rows(queries, mid_stride)
    kv_mid = jnp.stack([sample_rows(keys, mid_stride), sample_rows(values_in, mid_stride)])
    bit_count = MID_RATE.bit_length() - 1
    bit_order = list(range(bit_count))
    mid_keys = kv_mid
    source_ids = jnp.reshape(my_index, (1,))
    for bit_pos in bit_order:
        partner_keys = from_partner(mid_keys, "seq", bit_pos)
        mid_keys = jnp.concatenate([mid_keys, partner_keys], axis=2)
        source_ids = jnp.concatenate([source_ids, source_ids ^ 1 << bit_pos])
    mid_owners = jnp.repeat(source_ids, mid_rows, total_repeat_length=mid_stride * mid_rows)
    mid_within = jnp.tile(jnp.arange(mid_rows, dtype=jnp.int32), mid_stride)
    mid_alive = key_alive(mid_owners, mid_within, counts, mid_stride, heads_n)
    mid_ctx, mid_lt = sampled_attention(q_mid, mid_keys, mid_alive, mid_stride, scale)
    wide_rows = tok_dev // seq_n
    q_wide = sample_rows(queries, seq_n)
    kv_wide = jnp.stack([sample_rows(keys, seq_n), sample_rows(values_in, seq_n)])
    wide_keys = lax.all_gather(kv_wide, "seq", axis=2, tiled=True)
    wide_owners = jnp.arange(seq_n * wide_rows, dtype=jnp.int32) // wide_rows
    wide_within = jnp.arange(seq_n * wide_rows, dtype=jnp.int32) % wide_rows
    wide_alive = key_alive(wide_owners, wide_within, counts, seq_n, heads_n)
    wide_ctx, wide_lt = sampled_attention(q_wide, wide_keys, wide_alive, seq_n, scale)
    mixed = combine([local_ctx, mid_ctx, wide_ctx], [local_lt, mid_lt, wide_lt])
    mixed = jnp.where(is_live[None, :, None], mixed, 0.0)
    return mixed.transpose(1, 0, 2).reshape(tok_dev, width).astype(jnp.bfloat16)[None]


MIB = 2**20


def pair_order(move):
    dp_n = lax.axis_size("dp")
    seq_n = lax.axis_size("seq")
    pairs = []
    for row in range(dp_n):
        for col in range(seq_n):
            to_row, to_col = move(row, col)
            pairs.append((row * seq_n + col, to_row * seq_n + to_col))
    return pairs


def route(value, move):
    return lax.ppermute(value, ("dp", "seq"), pair_order(move))


def core_swap(value):
    return route(value, lambda row, col: (row, col ^ 1))


def chip_swap(value):
    return route(value, lambda row, col: (row, col ^ 2))


def my_half():
    return lax.axis_index("seq") // 2


def my_core():
    return lax.axis_index("seq") % 2


def columns_kernel(weight_ref, mine_ref, part_ref, sems):
    cols_n = mine_ref.shape[1]
    part_n = part_ref.shape[0]
    third = cols_n // 3
    half = my_half()
    copies = []
    for kind in range(3):
        start = pl.multiple_of((2 * kind + half) * third, third)
        copies.append(
            pltpu.make_async_copy(
                weight_ref.at[:, pl.ds(start, third)],
                mine_ref.at[:, pl.ds(kind * third, third)],
                sems.at[kind],
            )
        )
    for copy in copies:
        copy.start()
    for copy in copies:
        copy.wait()
    first = pl.multiple_of(my_core() * part_n, part_n)
    part_ref[...] = mine_ref[pl.ds(first, part_n), :]


def my_columns(weight):
    rows_n, width3 = weight.shape
    cols_n = width3 // 2
    return pl.pallas_call(
        columns_kernel,
        in_specs=[pl.BlockSpec(memory_space=pl.ANY)],
        out_specs=[pl.BlockSpec(memory_space=pltpu.VMEM)] * 2,
        out_shape=[
            jax.ShapeDtypeStruct((rows_n, cols_n), weight.dtype),
            jax.ShapeDtypeStruct((rows_n // 2, cols_n), weight.dtype),
        ],
        scratch_shapes=[pltpu.SemaphoreType.DMA((3,))],
        compiler_params=pltpu.CompilerParams(vmem_limit_bytes=4 * MIB),
        cost_estimate=pl.CostEstimate(
            flops=0, transcendentals=0, bytes_accessed=5 * rows_n * cols_n
        ),
        name="my_columns",
    )(weight)


def gather_columns(weight):
    own, part = my_columns(weight)
    near = route(own, lambda row, col: (row ^ (4 if col & 1 else 2), col))
    side = route(part, lambda row, col: (row ^ 1, col))
    cross = route(near, lambda row, col: (row ^ 1, col))
    far = route(near, lambda row, col: (row ^ (2 if col & 1 else 0), col))
    corner = route(side, lambda row, col: (row ^ 6, col))
    return (
        own,
        near,
        core_swap(near),
        cross,
        core_swap(cross),
        far,
        core_swap(far),
        side,
        core_swap(side),
        corner,
        core_swap(corner),
    )


def project_kernel(rows_ref, gain_ref, *refs):
    own, near, near2, cross, cross2, far, far2, side, side2, corner, corner2 = refs[:11]
    out_ref, query_ref, pair_ref, weight_scr, total_scr, sems = refs[11:]
    shard = own.shape[0]
    part = side.shape[0]
    mine = lax.axis_index("dp")
    core = my_core()
    half = my_half()

    def shard_at(mask):
        return pl.multiple_of(jnp.bitwise_xor(mine, mask) * shard, shard)

    copies = []

    def put(source, first):
        copies.append((source, weight_scr.at[pl.ds(first, source.shape[0]), :]))

    put(own, shard_at(0))
    put(near, shard_at(2 + 2 * core))
    put(near2, shard_at(4 - 2 * core))
    put(cross, shard_at(3 + 2 * core))
    put(cross2, shard_at(5 - 2 * core))
    low = core * part
    high = part - core * part
    put(side, pl.multiple_of(shard_at(1) + low, part))
    put(side2, pl.multiple_of(shard_at(1) + high, part))
    put(corner, pl.multiple_of(shard_at(7) + low, part))
    put(corner2, pl.multiple_of(shard_at(7) + high, part))
    handles = []
    for pos, (source, target) in enumerate(copies):
        handles.append(pltpu.make_async_copy(source, target, sems.at[pos]))
        handles[-1].start()
    far_at = weight_scr.at[pl.ds(shard_at(6), shard), :]

    @pl.when(core == 1)
    def _():
        pltpu.make_async_copy(far, far_at, sems.at[len(copies)]).start()

    @pl.when(core == 0)
    def _():
        pltpu.make_async_copy(far2, far_at, sems.at[len(copies)]).start()

    handles.append(pltpu.make_async_copy(far, far_at, sems.at[len(copies)]))
    normed = layer_norm(rows_ref[...], gain_ref[...])
    for handle in handles:
        handle.wait()
    total = jnp.dot(normed, weight_scr[...], preferred_element_type=jnp.float32)
    out_ref[...] = total.astype(jnp.bfloat16)
    heads_n, samp_n, head_dim = query_ref.shape
    stride = total.shape[0] // samp_n
    for kind in range(3):
        for head in range(heads_n):
            slot = kind * heads_n + head
            total_scr[slot] = total[:, slot * head_dim : (slot + 1) * head_dim]
            offset = lax.rem(half * heads_n + head, stride)
            picked = total_scr.at[slot][pl.ds(offset, samp_n, stride=stride), :]
            if kind == 0:
                query_ref[head] = picked.astype(jnp.bfloat16)
            else:
                pair_ref[kind - 1, head] = picked.astype(jnp.bfloat16)


def project(rows_in, gain, pieces, heads_n, stride):
    rows_n, depth = rows_in.shape
    cols_n = pieces[0].shape[1]
    head_dim = cols_n // (3 * heads_n)
    samp_n = rows_n // stride
    return pl.pallas_call(
        project_kernel,
        in_specs=[pl.BlockSpec(memory_space=pltpu.VMEM)] * 2
        + [pl.BlockSpec(memory_space=pl.ANY)] * len(pieces),
        out_specs=[pl.BlockSpec(memory_space=pltpu.VMEM)] * 3,
        out_shape=[
            jax.ShapeDtypeStruct((rows_n, cols_n), jnp.bfloat16),
            jax.ShapeDtypeStruct((heads_n, samp_n, head_dim), jnp.bfloat16),
            jax.ShapeDtypeStruct((2, heads_n, samp_n, head_dim), jnp.bfloat16),
        ],
        scratch_shapes=[
            pltpu.VMEM((depth, cols_n), jnp.bfloat16),
            pltpu.VMEM((3 * heads_n, rows_n, head_dim), jnp.float32),
            pltpu.SemaphoreType.DMA((10,)),
        ],
        compiler_params=pltpu.CompilerParams(vmem_limit_bytes=20 * MIB),
        cost_estimate=pl.CostEstimate(
            flops=2 * rows_n * depth * cols_n,
            transcendentals=0,
            bytes_accessed=2 * (rows_n * depth + depth * cols_n + rows_n * cols_n),
        ),
    )(rows_in, gain, *pieces)


def row_times(left, right):
    return lax.dot_general(
        left, right, (((1,), (1,)), ((), ())), preferred_element_type=jnp.float32
    )


def attend_kernel(stride, mine_first, parts_n, keys_at, counts_ref, *refs):
    qkv_refs = refs[:parts_n]
    query_refs = refs[parts_n : 2 * parts_n]
    pair_refs = refs[2 * parts_n : 2 * parts_n + len(keys_at)]
    rest = refs[2 * parts_n + len(keys_at) :]
    if mine_first:
        out_ref, full_scr, kept_scr, sem = rest
    else:
        out_ref, full_scr = rest
        kept_scr = out_ref
    heads_n, _, head_dim = query_refs[0].shape
    tok_dev = full_scr.shape[1]
    width = heads_n * head_dim
    half = my_half()
    seq_index = lax.axis_index("seq")
    block = seq_index if mine_first else jnp.bitwise_xor(seq_index, 2)
    factor = head_dim ** (-0.5) * math.log2(math.e)
    live_n = counts_ref[0, block]
    key_slot = lax.broadcasted_iota(jnp.int32, (1, tok_dev), 1)
    local_bias = jnp.where(key_slot < live_n, 0.0, NEG)
    row_live = lax.broadcasted_iota(jnp.int32, (tok_dev, head_dim), 0) < live_n

    def gathered(column):
        return jnp.concatenate(
            [ref[:, column * head_dim : (column + 1) * head_dim] for ref in qkv_refs]
        )

    for head in range(heads_n):
        query = gathered(head)
        key = gathered(heads_n + head)
        value = gathered(2 * heads_n + head)
        scores = row_times(query, key) + local_bias
        top = jnp.max(scores, axis=-1, keepdims=True)
        expo = jnp.exp2((scores - top) * factor)
        denom = jnp.sum(expo, axis=-1, keepdims=True)
        result = jnp.dot(expo.astype(jnp.bfloat16), value, preferred_element_type=jnp.float32)
        full_scr[head] = result / denom
        offset = lax.rem(half * heads_n + head, stride)
        live_parts = []
        for (mask, first), ref in zip(keys_at, pair_refs):
            samp_slot = lax.broadcasted_iota(jnp.int32, (1, ref.shape[2]), 1)
            slots = first + offset + stride * samp_slot
            owner = jnp.bitwise_xor(seq_index, mask)
            live_parts.append(jnp.where(slots < counts_ref[0, owner], 0.0, NEG))
        samp_bias = jnp.concatenate(live_parts, axis=1)
        samp_query = jnp.concatenate([ref[head] for ref in query_refs])
        samp_keys = jnp.concatenate([ref[0, head] for ref in pair_refs])
        samp_values = jnp.concatenate([ref[1, head] for ref in pair_refs])
        near_scores = row_times(samp_query, key) + local_bias
        wide_scores = row_times(samp_query, samp_keys) + samp_bias
        top = jnp.maximum(
            jnp.max(near_scores, axis=-1, keepdims=True),
            jnp.max(wide_scores, axis=-1, keepdims=True),
        )
        near = jnp.exp2((near_scores - top) * factor)
        wide = jnp.exp2((wide_scores - top) * factor)
        denom = jnp.sum(near, axis=-1, keepdims=True) + 2.0 * jnp.sum(
            wide, axis=-1, keepdims=True
        )
        result = jnp.dot(
            near.astype(jnp.bfloat16), value, preferred_element_type=jnp.float32
        ) + 2.0 * jnp.dot(
            wide.astype(jnp.bfloat16), samp_values, preferred_element_type=jnp.float32
        )
        samp_n = samp_query.shape[0]
        full_scr.at[head][pl.ds(offset, samp_n, stride=stride), :] = result / denom
        kept_scr[:, head * head_dim : (head + 1) * head_dim] = jnp.where(
            row_live, full_scr[head], 0.0
        ).astype(jnp.bfloat16)
    if mine_first:
        at = pl.multiple_of(half * width, width)
        copy = pltpu.make_async_copy(kept_scr, out_ref.at[:, pl.ds(at, width)], sem)
        copy.start()
        copy.wait()


def attend_block(counts, parts, keys, stride, mine_first):
    qkvs = [part[0] for part in parts]
    queries = [part[1] for part in parts]
    pairs = [pair for _, _, pair in keys]
    keys_at = tuple((mask, first) for mask, first, _ in keys)
    tok_dev = sum(qkv.shape[0] for qkv in qkvs)
    heads_n, _, head_dim = queries[0].shape
    width = heads_n * head_dim
    scratch = [pltpu.VMEM((heads_n, tok_dev, head_dim), jnp.float32)]
    if mine_first:
        scratch += [pltpu.VMEM((tok_dev, width), jnp.bfloat16), pltpu.SemaphoreType.DMA]
    return pl.pallas_call(
        functools.partial(attend_kernel, stride, mine_first, len(parts), keys_at),
        in_specs=[pl.BlockSpec(memory_space=pltpu.SMEM)]
        + [pl.BlockSpec(memory_space=pltpu.VMEM)] * (2 * len(parts) + len(keys)),
        out_specs=pl.BlockSpec(memory_space=pl.ANY if mine_first else pltpu.VMEM),
        out_shape=jax.ShapeDtypeStruct(
            (tok_dev, width * (2 if mine_first else 1)), jnp.bfloat16
        ),
        scratch_shapes=scratch,
        compiler_params=pltpu.CompilerParams(vmem_limit_bytes=16 * MIB),
        cost_estimate=pl.CostEstimate(
            flops=5 * heads_n * tok_dev * tok_dev * head_dim,
            transcendentals=2 * heads_n * tok_dev * tok_dev,
            bytes_accessed=8 * tok_dev * width,
        ),
        name="attend_mine" if mine_first else "attend_other",
    )(counts, *qkvs, *queries, *pairs)


def join_kernel(other_ref, _, out_ref, sem):
    width = other_ref.shape[1]
    at = pl.multiple_of((1 - my_half()) * width, width)
    copy = pltpu.make_async_copy(other_ref, out_ref.at[:, pl.ds(at, width)], sem)
    copy.start()
    copy.wait()


def join_halves(kept, other):
    return pl.pallas_call(
        join_kernel,
        in_specs=[pl.BlockSpec(memory_space=pltpu.VMEM), pl.BlockSpec(memory_space=pl.ANY)],
        out_specs=pl.BlockSpec(memory_space=pl.ANY),
        out_shape=jax.ShapeDtypeStruct(kept.shape, kept.dtype),
        scratch_shapes=[pltpu.SemaphoreType.DMA],
        input_output_aliases={1: 0},
        compiler_params=pltpu.CompilerParams(vmem_limit_bytes=2 * MIB),
        cost_estimate=pl.CostEstimate(flops=0, transcendentals=0, bytes_accessed=4 * other.size),
        name="join_halves",
    )(other, kept)


def local_paired(tiles, tile_counts, norm_gain, qkv_weight):
    return paired_layer(tiles, tile_counts, norm_gain, qkv_weight)


def paired_layer(tiles, tile_counts, norm_gain, qkv_weight):
    rows_in = tiles[0]
    tok_dev = rows_in.shape[0]
    stride = MID_RATE
    heads_n = HEADS // 2
    gain = norm_gain[None]
    cut = 2 * tok_dev // 3
    first = chip_swap(rows_in[:cut])
    second = chip_swap(rows_in[cut:])
    pieces = gather_columns(qkv_weight)
    qkv, query, pair = project(rows_in, gain, pieces, heads_n, stride)
    pair_r = core_swap(pair)
    qkv_a, query_a, pair_a = project(first, gain, pieces, heads_n, stride)
    pair_ar = core_swap(pair_a)
    qkv_b, query_b, pair_b = project(second, gain, pieces, heads_n, stride)
    pair_br = core_swap(pair_b)
    keys = [
        (0, 0, pair),
        (2, 0, pair_a),
        (2, cut, pair_b),
        (1, 0, pair_r),
        (3, 0, pair_ar),
        (3, cut, pair_br),
    ]
    other = attend_block(
        tile_counts, [(qkv_a, query_a), (qkv_b, query_b)], keys, stride, False
    )
    back = chip_swap(other)
    kept = attend_block(tile_counts, [(qkv, query)], keys, stride, True)
    return join_halves(kept, back)[None]


def solution(mesh):
    paired = (
        mesh.shape["seq"] == MID_RATE == 4 and mesh.shape["dp"] == 8 and HEADS % 2 == 0
    )
    return jax.shard_map(
        local_paired if paired else local,
        mesh=mesh,
        in_specs=(P("dp", "seq", None), P("dp", None), P(), P("dp", None)),
        out_specs=P("dp", "seq", None),
        check_vma=False,
    )
```

```python
import functools
import math

import jax
import jax.numpy as jnp
from jax import lax
from jax.experimental import pallas as pl
from jax.experimental.pallas import tpu as pltpu
from jax.sharding import PartitionSpec as P

HEADS = 6
MID_RATE = 4


NEG = -1e30
EPS = 1e-05


def from_partner(value, axis, bit):
    mask = 2**bit
    pairs = [(source, source ^ mask) for source in range(lax.axis_size(axis))]
    return lax.ppermute(value, axis, pairs)


def layer_norm(rows_in, gain):
    floats = rows_in.astype(jnp.float32)
    center = floats - jnp.mean(floats, axis=-1, keepdims=True)
    spread_sq = jnp.mean(center * center, axis=-1, keepdims=True)
    return (center * lax.rsqrt(spread_sq + EPS) * gain).astype(jnp.bfloat16)


def sample_rows(array, stride):
    shaped = array.reshape((array.shape[0] // stride, stride) + array.shape[1:])
    return jnp.stack([shaped[:, head_idx % stride, head_idx] for head_idx in range(array.shape[1])])


def attend(queries, keys, values_in, key_live, scale):
    scores = (
        jnp.einsum("hsqd,hskd->hsqk", queries, keys, preferred_element_type=jnp.float32) * scale
    )
    scores = jnp.where(key_live[:, :, None, :], scores, NEG)
    top = jnp.max(scores, axis=-1)
    expo = jnp.exp(scores - top[..., None])
    denom = jnp.sum(expo, axis=-1)
    weights = (expo / denom[..., None]).astype(jnp.bfloat16)
    result = jnp.einsum("hsqk,hskd->hsqd", weights, values_in, preferred_element_type=jnp.float32)
    return (result, top + jnp.log(denom))


def spread(result, log_total, stride):
    heads_n = result.shape[0]
    count_n = result.shape[1]
    onehot = (
        jnp.arange(stride, dtype=jnp.int32)[None, :]
        == (jnp.arange(heads_n, dtype=jnp.int32) % stride)[:, None]
    )
    full_ctx = (result[:, :, None, :] * onehot[:, None, :, None].astype(result.dtype)).reshape(
        heads_n, count_n * stride, result.shape[2]
    )
    chosen = jnp.broadcast_to(onehot[:, None, :], (heads_n, count_n, stride)).reshape(
        heads_n, count_n * stride
    )
    full_lt = jnp.where(chosen, jnp.repeat(log_total, stride, axis=1), NEG)
    return (full_ctx, full_lt)


def combine(contexts, totals):
    stacked_lt = jnp.stack(totals)
    top = jnp.max(stacked_lt, axis=0)
    wts = jnp.exp(stacked_lt - top)
    stacked_ctx = jnp.stack(contexts)
    return jnp.sum(wts[..., None] * stacked_ctx, axis=0) / jnp.sum(wts, axis=0)[..., None]


def key_alive(owners, within, counts, stride, heads_n):
    seq_n = counts.shape[0]
    owner_count = jnp.sum(
        jnp.where(
            owners[:, None] == jnp.arange(seq_n, dtype=jnp.int32)[None, :], counts[None, :], 0
        ),
        axis=1,
    )
    offsets = jnp.arange(heads_n, dtype=jnp.int32) % stride
    slots = offsets[:, None] + stride * within[None, :]
    return slots < owner_count[None, :]


def sampled_attention(queries, gathered, alive, stride, scale):
    heads_n = queries.shape[0]
    per_dev = queries.shape[1]
    result, log_total = attend(
        queries[:, None], gathered[0][:, None], gathered[1][:, None], alive[:, None], scale
    )
    return spread(
        result.reshape(heads_n, per_dev, result.shape[3]),
        log_total.reshape(heads_n, per_dev),
        stride,
    )


def local(tiles, tile_counts, norm_gain, qkv_weight):
    rows_in = tiles[0]
    counts = tile_counts[0]
    tok_dev = rows_in.shape[0]
    seq_n = lax.axis_size("seq")
    my_index = lax.axis_index("seq")
    dev_ids = jnp.arange(seq_n, dtype=jnp.int32)
    my_count = jnp.sum(jnp.where(dev_ids == my_index, counts, 0))
    is_live = jnp.arange(tok_dev, dtype=jnp.int32) < my_count
    normed = layer_norm(rows_in, norm_gain)
    width3 = qkv_weight.shape[1]
    width = width3 // 3
    heads_n = HEADS
    head_dim = width // heads_n
    scale = head_dim ** (-0.5)
    qkv = jnp.dot(
        normed,
        lax.all_gather(qkv_weight, "dp", axis=0, tiled=True),
        preferred_element_type=jnp.float32,
    ).astype(jnp.bfloat16)
    queries = qkv[:, :width].reshape(tok_dev, heads_n, head_dim)
    keys = qkv[:, width : 2 * width].reshape(tok_dev, heads_n, head_dim)
    values_in = qkv[:, 2 * width :].reshape(tok_dev, heads_n, head_dim)
    local_live = jnp.broadcast_to(is_live[None, None, :], (heads_n, 1, tok_dev))
    local_ctx, local_lt = attend(
        queries.transpose(1, 0, 2)[:, None],
        keys.transpose(1, 0, 2)[:, None],
        values_in.transpose(1, 0, 2)[:, None],
        local_live,
        scale,
    )
    local_ctx = local_ctx.reshape(heads_n, tok_dev, head_dim)
    local_lt = local_lt.reshape(heads_n, tok_dev)
    mid_stride = MID_RATE
    mid_rows = tok_dev // mid_stride
    q_mid = sample_rows(queries, mid_stride)
    kv_mid = jnp.stack([sample_rows(keys, mid_stride), sample_rows(values_in, mid_stride)])
    bit_count = MID_RATE.bit_length() - 1
    bit_order = list(range(bit_count))
    mid_keys = kv_mid
    source_ids = jnp.reshape(my_index, (1,))
    for bit_pos in bit_order:
        partner_keys = from_partner(mid_keys, "seq", bit_pos)
        mid_keys = jnp.concatenate([mid_keys, partner_keys], axis=2)
        source_ids = jnp.concatenate([source_ids, source_ids ^ 1 << bit_pos])
    mid_owners = jnp.repeat(source_ids, mid_rows, total_repeat_length=mid_stride * mid_rows)
    mid_within = jnp.tile(jnp.arange(mid_rows, dtype=jnp.int32), mid_stride)
    mid_alive = key_alive(mid_owners, mid_within, counts, mid_stride, heads_n)
    mid_ctx, mid_lt = sampled_attention(q_mid, mid_keys, mid_alive, mid_stride, scale)
    wide_rows = tok_dev // seq_n
    q_wide = sample_rows(queries, seq_n)
    kv_wide = jnp.stack([sample_rows(keys, seq_n), sample_rows(values_in, seq_n)])
    wide_keys = lax.all_gather(kv_wide, "seq", axis=2, tiled=True)
    wide_owners = jnp.arange(seq_n * wide_rows, dtype=jnp.int32) // wide_rows
    wide_within = jnp.arange(seq_n * wide_rows, dtype=jnp.int32) % wide_rows
    wide_alive = key_alive(wide_owners, wide_within, counts, seq_n, heads_n)
    wide_ctx, wide_lt = sampled_attention(q_wide, wide_keys, wide_alive, seq_n, scale)
    mixed = combine([local_ctx, mid_ctx, wide_ctx], [local_lt, mid_lt, wide_lt])
    mixed = jnp.where(is_live[None, :, None], mixed, 0.0)
    return mixed.transpose(1, 0, 2).reshape(tok_dev, width).astype(jnp.bfloat16)[None]


MIB = 2**20


def pair_order(move):
    dp_n = lax.axis_size("dp")
    seq_n = lax.axis_size("seq")
    pairs = []
    for row in range(dp_n):
        for col in range(seq_n):
            to_row, to_col = move(row, col)
            pairs.append((row * seq_n + col, to_row * seq_n + to_col))
    return pairs


def route(value, move):
    return lax.ppermute(value, ("dp", "seq"), pair_order(move))


def core_swap(value):
    return route(value, lambda row, col: (row, col ^ 1))


def chip_swap(value):
    return route(value, lambda row, col: (row, col ^ 2))


def my_half():
    return lax.axis_index("seq") // 2


def my_core():
    return lax.axis_index("seq") % 2


def prepare_kernel(rows_ref, weight_ref, first_ref, second_ref, mine_ref, part_ref, sems):
    cut = first_ref.shape[0]
    part_n, cols_n = part_ref.shape
    third = cols_n // 3
    half = my_half()
    top = pl.multiple_of(my_core() * part_n, part_n)
    pairs = []
    for kind in range(3):
        columns = pl.ds(pl.multiple_of((2 * kind + half) * third, third), third)
        target = pl.ds(kind * third, third)
        pairs.append((weight_ref.at[pl.ds(top, part_n), columns], part_ref.at[:, target]))
        pairs.append((weight_ref.at[:, columns], mine_ref.at[:, target]))
    pairs.append((rows_ref.at[pl.ds(0, cut), :], first_ref))
    pairs.append((rows_ref.at[pl.ds(cut, second_ref.shape[0]), :], second_ref))
    copies = [
        pltpu.make_async_copy(source, target, sems.at[pos])
        for pos, (source, target) in enumerate(pairs)
    ]
    for copy in copies:
        copy.start()
    for copy in copies:
        copy.wait()


def prepare(rows_in, weight, cut):
    tok_dev, depth = rows_in.shape
    rows_n, width3 = weight.shape
    cols_n = width3 // 2
    return pl.pallas_call(
        prepare_kernel,
        in_specs=[pl.BlockSpec(memory_space=pl.ANY)] * 2,
        out_specs=[pl.BlockSpec(memory_space=pltpu.VMEM)] * 4,
        out_shape=[
            jax.ShapeDtypeStruct((cut, depth), rows_in.dtype),
            jax.ShapeDtypeStruct((tok_dev - cut, depth), rows_in.dtype),
            jax.ShapeDtypeStruct((rows_n, cols_n), weight.dtype),
            jax.ShapeDtypeStruct((rows_n // 2, cols_n), weight.dtype),
        ],
        scratch_shapes=[pltpu.SemaphoreType.DMA((8,))],
        compiler_params=pltpu.CompilerParams(vmem_limit_bytes=1 * MIB),
        cost_estimate=pl.CostEstimate(
            flops=0, transcendentals=0, bytes_accessed=4 * rows_in.size + 5 * rows_n * cols_n
        ),
        name="prepare",
    )(rows_in, weight)


def gather_columns(part):
    found = {}
    found[4] = route(part, lambda row, col: (row ^ 4, col))
    found[2] = route(part, lambda row, col: (row ^ 2, col))
    found[1] = route(part, lambda row, col: (row ^ 1, col))
    found[7] = route(found[1], lambda row, col: (row ^ 6, col))
    found[3] = route(found[2], lambda row, col: (row ^ 1, col))
    found[5] = route(found[4], lambda row, col: (row ^ 1, col))
    found[6] = route(found[4], lambda row, col: (row ^ 2, col))
    masks = sorted(found)
    return [found[mask] for mask in masks] + [core_swap(found[mask]) for mask in masks]


def norm_kernel(first_ref, second_ref, gain_ref, out_ref):
    cut = first_ref.shape[0]
    out_ref[:cut] = layer_norm(first_ref[...], gain_ref[...])
    out_ref[cut:] = layer_norm(second_ref[...], gain_ref[...])


def norm_rows(first, second, gain):
    depth = first.shape[1]
    rows_n = first.shape[0] + second.shape[0]
    return pl.pallas_call(
        norm_kernel,
        in_specs=[pl.BlockSpec(memory_space=pltpu.VMEM)] * 3,
        out_specs=pl.BlockSpec(memory_space=pltpu.VMEM),
        out_shape=jax.ShapeDtypeStruct((rows_n, depth), jnp.bfloat16),
        compiler_params=pltpu.CompilerParams(vmem_limit_bytes=8 * MIB),
        cost_estimate=pl.CostEstimate(
            flops=8 * rows_n * depth, transcendentals=rows_n, bytes_accessed=4 * rows_n * depth
        ),
        name="norm_mine",
    )(first, second, gain)


def split_heads(total, query_ref, pair_ref, out_ref, total_scr):
    out_ref[...] = total.astype(jnp.bfloat16)
    heads_n, samp_n, head_dim = query_ref.shape
    stride = total.shape[0] // samp_n
    half = my_half()
    for kind in range(3):
        for head in range(heads_n):
            slot = kind * heads_n + head
            total_scr[slot] = total[:, slot * head_dim : (slot + 1) * head_dim]
            offset = lax.rem(half * heads_n + head, stride)
            picked = total_scr.at[slot][pl.ds(offset, samp_n, stride=stride), :]
            if kind == 0:
                query_ref[head] = picked.astype(jnp.bfloat16)
            else:
                pair_ref[kind - 1, head] = picked.astype(jnp.bfloat16)


def project_mine_kernel(rows_ref, own_ref, *refs):
    pieces_n = len(refs) - 5
    pieces = refs[:pieces_n]
    weight_ref, out_ref, query_ref, pair_ref, total_scr = refs[pieces_n:]
    shard = own_ref.shape[0]
    part = pieces[0].shape[0]
    mine = lax.axis_index("dp")
    core = my_core()
    weight_ref[pl.ds(pl.multiple_of(mine * shard, shard), shard), :] = own_ref[...]
    for pos, piece in enumerate(pieces):
        mask = pos % (pieces_n // 2) + 1
        holder = core if pos < pieces_n // 2 else 1 - core
        first = jnp.bitwise_xor(mine, mask) * shard + holder * part
        weight_ref[pl.ds(pl.multiple_of(first, part), part), :] = piece[...]
    total = jnp.dot(rows_ref[...], weight_ref[...], preferred_element_type=jnp.float32)
    split_heads(total, query_ref, pair_ref, out_ref, total_scr)


def project_kernel(rows_ref, gain_ref, weight_ref, out_ref, query_ref, pair_ref, total_scr):
    normed = layer_norm(rows_ref[...], gain_ref[...])
    total = jnp.dot(normed, weight_ref[...], preferred_element_type=jnp.float32)
    split_heads(total, query_ref, pair_ref, out_ref, total_scr)


def project_call(kernel, rows_n, cols_n, depth, heads_n, stride, with_weight, args):
    head_dim = cols_n // (3 * heads_n)
    samp_n = rows_n // stride
    shapes = [
        jax.ShapeDtypeStruct((rows_n, cols_n), jnp.bfloat16),
        jax.ShapeDtypeStruct((heads_n, samp_n, head_dim), jnp.bfloat16),
        jax.ShapeDtypeStruct((2, heads_n, samp_n, head_dim), jnp.bfloat16),
    ]
    if with_weight:
        shapes = [jax.ShapeDtypeStruct((depth, cols_n), jnp.bfloat16)] + shapes
    return pl.pallas_call(
        kernel,
        in_specs=[pl.BlockSpec(memory_space=pltpu.VMEM)] * len(args),
        out_specs=[pl.BlockSpec(memory_space=pltpu.VMEM)] * len(shapes),
        out_shape=shapes,
        scratch_shapes=[pltpu.VMEM((3 * heads_n, rows_n, head_dim), jnp.float32)],
        compiler_params=pltpu.CompilerParams(vmem_limit_bytes=16 * MIB),
        cost_estimate=pl.CostEstimate(
            flops=2 * rows_n * depth * cols_n,
            transcendentals=0,
            bytes_accessed=2 * (rows_n * depth + depth * cols_n + rows_n * cols_n),
        ),
    )(*args)


def row_times(left, right):
    return lax.dot_general(
        left, right, (((1,), (1,)), ((), ())), preferred_element_type=jnp.float32
    )


def attend_kernel(stride, mine_first, parts_n, keys_at, counts_ref, *refs):
    qkv_refs = refs[:parts_n]
    query_refs = refs[parts_n : 2 * parts_n]
    pair_refs = refs[2 * parts_n : 2 * parts_n + len(keys_at)]
    rest = refs[2 * parts_n + len(keys_at) :]
    if mine_first:
        out_ref, full_scr, kept_scr, sem = rest
    else:
        out_ref, full_scr = rest
        kept_scr = out_ref
    heads_n, _, head_dim = query_refs[0].shape
    tok_dev = full_scr.shape[1]
    width = heads_n * head_dim
    half = my_half()
    seq_index = lax.axis_index("seq")
    block = seq_index if mine_first else jnp.bitwise_xor(seq_index, 2)
    factor = head_dim ** (-0.5) * math.log2(math.e)
    live_n = counts_ref[0, block]
    key_slot = lax.broadcasted_iota(jnp.int32, (1, tok_dev), 1)
    local_bias = jnp.where(key_slot < live_n, 0.0, NEG)
    row_live = lax.broadcasted_iota(jnp.int32, (tok_dev, head_dim), 0) < live_n

    def gathered(column):
        return jnp.concatenate(
            [ref[:, column * head_dim : (column + 1) * head_dim] for ref in qkv_refs]
        )

    for head in range(heads_n):
        query = gathered(head)
        key = gathered(heads_n + head)
        value = gathered(2 * heads_n + head)
        scores = row_times(query, key) + local_bias
        top = jnp.max(scores, axis=-1, keepdims=True)
        expo = jnp.exp2((scores - top) * factor)
        denom = jnp.sum(expo, axis=-1, keepdims=True)
        result = jnp.dot(expo.astype(jnp.bfloat16), value, preferred_element_type=jnp.float32)
        full_scr[head] = result / denom
        offset = lax.rem(half * heads_n + head, stride)
        live_parts = []
        for (mask, first), ref in zip(keys_at, pair_refs):
            samp_slot = lax.broadcasted_iota(jnp.int32, (1, ref.shape[2]), 1)
            slots = first + offset + stride * samp_slot
            owner = jnp.bitwise_xor(seq_index, mask)
            live_parts.append(jnp.where(slots < counts_ref[0, owner], 0.0, NEG))
        samp_bias = jnp.concatenate(live_parts, axis=1)
        samp_query = jnp.concatenate([ref[head] for ref in query_refs])
        samp_keys = jnp.concatenate([ref[0, head] for ref in pair_refs])
        samp_values = jnp.concatenate([ref[1, head] for ref in pair_refs])
        near_scores = row_times(samp_query, key) + local_bias
        wide_scores = row_times(samp_query, samp_keys) + samp_bias
        top = jnp.maximum(
            jnp.max(near_scores, axis=-1, keepdims=True),
            jnp.max(wide_scores, axis=-1, keepdims=True),
        )
        near = jnp.exp2((near_scores - top) * factor)
        wide = jnp.exp2((wide_scores - top) * factor)
        denom = jnp.sum(near, axis=-1, keepdims=True) + 2.0 * jnp.sum(
            wide, axis=-1, keepdims=True
        )
        result = jnp.dot(
            near.astype(jnp.bfloat16), value, preferred_element_type=jnp.float32
        ) + 2.0 * jnp.dot(
            wide.astype(jnp.bfloat16), samp_values, preferred_element_type=jnp.float32
        )
        samp_n = samp_query.shape[0]
        full_scr.at[head][pl.ds(offset, samp_n, stride=stride), :] = result / denom
        kept_scr[:, head * head_dim : (head + 1) * head_dim] = jnp.where(
            row_live, full_scr[head], 0.0
        ).astype(jnp.bfloat16)
    if mine_first:
        at = pl.multiple_of(half * width, width)
        copy = pltpu.make_async_copy(kept_scr, out_ref.at[:, pl.ds(at, width)], sem)
        copy.start()
        copy.wait()


def attend_block(counts, parts, keys, stride, mine_first):
    qkvs = [part[0] for part in parts]
    queries = [part[1] for part in parts]
    pairs = [pair for _, _, pair in keys]
    keys_at = tuple((mask, first) for mask, first, _ in keys)
    tok_dev = sum(qkv.shape[0] for qkv in qkvs)
    heads_n, _, head_dim = queries[0].shape
    width = heads_n * head_dim
    scratch = [pltpu.VMEM((heads_n, tok_dev, head_dim), jnp.float32)]
    if mine_first:
        scratch += [pltpu.VMEM((tok_dev, width), jnp.bfloat16), pltpu.SemaphoreType.DMA]
    return pl.pallas_call(
        functools.partial(attend_kernel, stride, mine_first, len(parts), keys_at),
        in_specs=[pl.BlockSpec(memory_space=pltpu.SMEM)]
        + [pl.BlockSpec(memory_space=pltpu.VMEM)] * (2 * len(parts) + len(keys)),
        out_specs=pl.BlockSpec(memory_space=pl.ANY if mine_first else pltpu.VMEM),
        out_shape=jax.ShapeDtypeStruct(
            (tok_dev, width * (2 if mine_first else 1)), jnp.bfloat16
        ),
        scratch_shapes=scratch,
        compiler_params=pltpu.CompilerParams(vmem_limit_bytes=16 * MIB),
        cost_estimate=pl.CostEstimate(
            flops=5 * heads_n * tok_dev * tok_dev * head_dim,
            transcendentals=2 * heads_n * tok_dev * tok_dev,
            bytes_accessed=8 * tok_dev * width,
        ),
        name="attend_mine" if mine_first else "attend_other",
    )(counts, *qkvs, *queries, *pairs)


def join_kernel(other_ref, _, out_ref, sem):
    width = other_ref.shape[1]
    at = pl.multiple_of((1 - my_half()) * width, width)
    copy = pltpu.make_async_copy(other_ref, out_ref.at[:, pl.ds(at, width)], sem)
    copy.start()
    copy.wait()


def join_halves(kept, other):
    return pl.pallas_call(
        join_kernel,
        in_specs=[pl.BlockSpec(memory_space=pltpu.VMEM), pl.BlockSpec(memory_space=pl.ANY)],
        out_specs=pl.BlockSpec(memory_space=pl.ANY),
        out_shape=jax.ShapeDtypeStruct(kept.shape, kept.dtype),
        scratch_shapes=[pltpu.SemaphoreType.DMA],
        input_output_aliases={1: 0},
        compiler_params=pltpu.CompilerParams(vmem_limit_bytes=2 * MIB),
        cost_estimate=pl.CostEstimate(flops=0, transcendentals=0, bytes_accessed=4 * other.size),
        name="join_halves",
    )(other, kept)


def local_paired(tiles, tile_counts, norm_gain, qkv_weight):
    return paired_layer(tiles, tile_counts, norm_gain, qkv_weight)


def paired_layer(tiles, tile_counts, gain, qkv_weight):
    rows_in = tiles[0]
    tok_dev, depth = rows_in.shape
    cols_n = qkv_weight.shape[1] // 2
    stride = MID_RATE
    heads_n = HEADS // 2
    cut = 2 * tok_dev // 3
    first, second, own, part = prepare(rows_in, qkv_weight, cut)
    other_a = chip_swap(first)
    other_b = chip_swap(second)
    pieces = gather_columns(part)
    normed = norm_rows(first, second, gain)
    weight, qkv, query, pair = project_call(
        project_mine_kernel, tok_dev, cols_n, depth, heads_n, stride, True,
        (normed, own, *pieces),
    )
    pair_r = core_swap(pair)
    qkv_a, query_a, pair_a = project_call(
        project_kernel, cut, cols_n, depth, heads_n, stride, False,
        (other_a, gain, weight),
    )
    pair_ar = core_swap(pair_a)
    qkv_b, query_b, pair_b = project_call(
        project_kernel, tok_dev - cut, cols_n, depth, heads_n, stride, False,
        (other_b, gain, weight),
    )
    pair_br = core_swap(pair_b)
    keys = [
        (0, 0, pair),
        (2, 0, pair_a),
        (2, cut, pair_b),
        (1, 0, pair_r),
        (3, 0, pair_ar),
        (3, cut, pair_br),
    ]
    other = attend_block(
        tile_counts, [(qkv_a, query_a), (qkv_b, query_b)], keys, stride, False
    )
    back = chip_swap(other)
    kept = attend_block(tile_counts, [(qkv, query)], keys, stride, True)
    return join_halves(kept, back)[None]


def solution(mesh):
    paired = (
        mesh.shape["seq"] == MID_RATE == 4 and mesh.shape["dp"] == 8 and HEADS % 2 == 0
    )
    return jax.shard_map(
        local_paired if paired else local,
        mesh=mesh,
        in_specs=(P("dp", "seq", None), P("dp", None), P(), P("dp", None)),
        out_specs=P("dp", "seq", None),
        check_vma=False,
    )
```
